32 devices in a mesh: sx: 8 (over y, x, core), sy: 4 (over z).
Axes of the slice: x: 2, y: 2, z: 4, core: 2. Of those that a mesh axis runs over, the one named last changes fastest.
Arguments:
- sources: bfloat16 [8, 4, 2, 64, 4096], P('sx', 'sy'), may hold values from -6 to 6
- translate_re: bfloat16 [4, 2, 2, 64, 64], replicated, may hold values from -0.375 to 0.375
- translate_im: bfloat16 [4, 2, 2, 64, 64], replicated, may hold values from -0.375 to 0.375
- frame_index: int32 [8, 4, 16], P('sx', 'sy'), may hold values from 0 to 4095
- velocity_index: int32 [8, 4, 256], P('sx', 'sy'), may hold values from 0 to 4095
- eval_re: bfloat16 [64, 64], replicated, may hold values from -1.5 to 1.5
- eval_im: bfloat16 [64, 64], replicated, may hold values from -1.5 to 1.5
- window: int32 [8, 4], P('sx', 'sy'), may hold values from 1 to 2
Outputs:
- smoothed: bfloat16 [64, 32, 4096], P('sx', 'sy')
The draws below stay inside these ranges and needn't reach their ends.
All inputs are finite; a program needn't handle non-finite values.
Results may differ from the reference program's by a relative error of at most 0.0076.
Values may be sent and summed in bfloat16 or wider, within the bound.
A program may use at most 64 MiB of HBM per device.

```python
import math
import jax
import jax.numpy as jnp
from jax import lax

K = 64
TILE = 8
LEVELS = 4
FRAMES = 16
VGRID = 4096
VEL_DEV = 256
COLS = 4096
PX = 8
PY = 4
TX = 64
TY = 32
N_SX = 8
N_SY = 4


def plant(result, stream_key, low, top_value):
    longest = result.shape.index(max(result.shape))
    spots = []
    for shift in (0, 1):
        where = [jax.random.randint(jax.random.fold_in(stream_key, axis), (), 0, length) for axis, length in enumerate(result.shape)]
        where[longest] = (where[longest] + shift) % result.shape[longest]
        spots.append(tuple(where))
    return result.at[spots[0]].set(low).at[spots[1]].set(top_value)


def levels(stream_key, shape, cuts, low, top_value):
    gain = 1.0
    for dim, parts in cuts:
        draws = jax.random.uniform(jax.random.fold_in(jax.random.fold_in(stream_key, 6), dim), (parts,), jnp.float32, low / len(cuts), top_value / len(cuts))
        gain = gain * jnp.repeat(jnp.exp(draws), shape[dim] // parts).reshape((-1,) + (1,) * (len(shape) - 1 - dim))
    return gain


def gaussian(rng, shape, scale, most, shards=(), kind=jnp.bfloat16):
    gain = levels(rng, shape, shards, -0.22, 0.18) if shards else 1.0
    drawn = jax.random.normal(rng, shape, jnp.float32) * scale * gain
    return jnp.minimum(jnp.maximum(drawn, -most), most).astype(kind)


def setup_inputs(seed: int = 0) -> dict:
    splits = jax.random.split(jax.random.key(seed), 9)
    sources = gaussian(splits[0], (PX, PY, 2, K, COLS), 1.0, 6.0, ((0, 8), (1, 4)))
    translate_re = gaussian(splits[1], (LEVELS, 2, 2, K, K), (4 * K) ** -0.5, 0.375)
    translate_im = gaussian(splits[2], (LEVELS, 2, 2, K, K), (4 * K) ** -0.5, 0.375)
    frame_index = plant(jax.random.randint(splits[3], (PX, PY, FRAMES), 0, VGRID), jax.random.fold_in(splits[3], 1), 0, VGRID - 1).astype(jnp.int32)
    velocity_index = plant(jax.random.randint(splits[4], (PX, PY, VEL_DEV), 0, VGRID), jax.random.fold_in(splits[4], 1), 0, VGRID - 1).astype(jnp.int32)
    eval_re = gaussian(splits[5], (TILE * TILE, K), (K // 4) ** -0.5, 1.5)
    eval_im = gaussian(splits[6], (TILE * TILE, K), (K // 4) ** -0.5, 1.5)
    window = plant(jax.random.randint(splits[7], (PX, PY), 1, 3), jax.random.fold_in(splits[7], 1), 1, 2).astype(jnp.int32)
    return dict(sources=sources, translate_re=translate_re, translate_im=translate_im, frame_index=frame_index, velocity_index=velocity_index, eval_re=eval_re, eval_im=eval_im, window=window)


TWO_PI = 2.0 * math.pi


def blocks(real_part, imag_part):
    upper = jnp.concatenate([real_part, -imag_part], axis=-1)
    lower = jnp.concatenate([imag_part, real_part], axis=-1)
    return jnp.concatenate([upper, lower], axis=-2)


def angles_of(frame_index, velocity_index, level_no):
    product = (frame_index[..., :, None] * velocity_index[..., None, :] * (level_no + 1)) % VGRID
    angles = (TWO_PI / VGRID) * product.astype(jnp.float32)
    return angles.reshape(angles.shape[:-2] + (COLS,))


def partner_of(state, axis_no, bit_pos):
    shape = state.shape
    count = shape[axis_no]
    stride = 2 ** bit_pos
    split_shape = shape[:axis_no] + (count // (2 * stride), 2, stride) + shape[axis_no + 1:]
    return jnp.flip(state.reshape(split_shape), axis=axis_no + 1).reshape(shape)


def reference(sources, translate_re, translate_im, frame_index, velocity_index, eval_re, eval_im, window):
    state = sources
    row_ids = jnp.arange(N_SX, dtype=jnp.int32)[:, None]
    col_ids = jnp.arange(N_SY, dtype=jnp.int32)[None, :]
    for level_no in range(LEVELS):
        axis_no = level_no % 2
        extent = N_SX if axis_no == 0 else N_SY
        bit_pos = int(extent).bit_length() - 2 - level_no // 2
        partner = partner_of(state, axis_no, bit_pos)
        device_ids = row_ids if axis_no == 0 else col_ids
        bits = jnp.broadcast_to((device_ids >> bit_pos) & 1, (N_SX, N_SY)).astype(jnp.int32)
        angles = angles_of(frame_index, velocity_index, level_no)
        cosine = jnp.cos(angles)
        sine_part = jnp.sin(angles)
        mats_self = blocks(translate_re[level_no][:, 0], translate_im[level_no][:, 0])
        mats_other = blocks(translate_re[level_no][:, 1], translate_im[level_no][:, 1])

        def advance(items):
            own_rows, other_rows, bit_row, cos_row, sin_row = items
            self_pick = mats_self[bit_row].astype(jnp.float32)
            other_pick = mats_other[bit_row].astype(jnp.float32)
            own_flat = own_rows.reshape(N_SY, 2 * K, COLS).astype(jnp.float32)
            other_flat = other_rows.reshape(N_SY, 2 * K, COLS).astype(jnp.float32)
            total = jnp.einsum('dij,djc->dic', self_pick, own_flat) + jnp.einsum('dij,djc->dic', other_pick, other_flat)
            real_total = total[:, :K]
            imag_total = total[:, K:]
            new_real = cos_row[:, None, :] * real_total - sin_row[:, None, :] * imag_total
            new_imag = sin_row[:, None, :] * real_total + cos_row[:, None, :] * imag_total
            return jnp.stack([new_real, new_imag], axis=1).astype(jnp.bfloat16)

        state = lax.map(advance, (state, partner, bits, cosine, sine_part))
    evaluate = jnp.concatenate([eval_re, -eval_im], axis=1).astype(jnp.float32)

    def render(state_row):
        flat_rows = state_row.reshape(N_SY, 2 * K, COLS).astype(jnp.float32)
        tiles = jnp.einsum('pk,ykc->ypc', evaluate, flat_rows).astype(jnp.bfloat16)
        return tiles.reshape(N_SY, TILE, TILE, COLS)

    tiles_all = lax.map(render, state)
    picture = jnp.transpose(tiles_all, (0, 2, 1, 3, 4)).reshape(TX, TY, COLS)
    padded = jnp.pad(picture, ((2, 2), (2, 2), (0, 0)))

    def smooth(row_id):
        values = lax.dynamic_slice_in_dim(padded, row_id * TILE, TILE + 4, 0).astype(jnp.float32)
        rows_near = values[1:-3] + values[2:-2] + values[3:-1]
        rows_far = rows_near + values[0:-4] + values[4:]
        box_near = rows_near[:, 1:-3] + rows_near[:, 2:-2] + rows_near[:, 3:-1]
        box_far = rows_far[:, 1:-3] + rows_far[:, 2:-2] + rows_far[:, 3:-1] + rows_far[:, 0:-4] + rows_far[:, 4:]
        widths = jnp.repeat(window[row_id], TILE)
        chosen = jnp.where(widths[None, :, None] == 2, box_far / 25.0, box_near / 9.0)
        return chosen.astype(jnp.bfloat16)

    smoothed = lax.map(smooth, jnp.arange(N_SX, dtype=jnp.int32))
    return smoothed.reshape(TX, TY, COLS)
```

```python
import functools
import math

import jax
import jax.numpy as jnp
from jax import lax
from jax.experimental import pallas as pl
from jax.experimental.pallas import tpu as pltpu
from jax.sharding import PartitionSpec as P

LEVELS = 4
VGRID = 4096


TWO_PI = 2.0 * math.pi


def swapped(block, axis, bit):
    count = lax.axis_size(axis)
    route = []
    for low in range(count):
        high = low | 1 << bit
        if high != low and high < count:
            route += [(low, high), (high, low)]
    return lax.ppermute(block, axis, route)


def with_halo(block, sides, width):
    for axis, dim in sides:
        count = lax.axis_size(axis)
        forward = [(i, i + 1) for i in range(count - 1)]
        backward = [(target, source) for source, target in forward]
        low = lax.ppermute(
            lax.slice_in_dim(block, block.shape[dim] - width, None, axis=dim), axis, forward
        )
        high = lax.ppermute(lax.slice_in_dim(block, 0, width, axis=dim), axis, backward)
        block = jnp.concatenate([low, block, high], axis=dim)
    return block


def blocks(real_part, imag_part):
    upper = jnp.concatenate([real_part, -imag_part], axis=-1)
    lower = jnp.concatenate([imag_part, real_part], axis=-1)
    return jnp.concatenate([upper, lower], axis=-2)


def on_device(
    sources, translate_re, translate_im, frame_index, velocity_index, eval_re, eval_im, window
):
    terms = sources.shape[3]
    columns = sources.shape[4]
    state_flat = sources[0, 0].reshape(2 * terms, columns)
    base_product = frame_index[0, 0][:, None] * velocity_index[0, 0][None, :]
    for level_no in range(LEVELS):
        if level_no % 2 == 0:
            bit_pos = lax.axis_size("sx").bit_length() - 2 - level_no // 2
            own_bit = lax.axis_index("sx") >> bit_pos & 1
        else:
            bit_pos = lax.axis_size("sy").bit_length() - 2 - level_no // 2
            own_bit = lax.axis_index("sy") >> bit_pos & 1
        self_matrix = blocks(translate_re[level_no, own_bit, 0], translate_im[level_no, own_bit, 0])
        own_part = jnp.dot(self_matrix, state_flat, preferred_element_type=jnp.float32)
        if level_no % 2 == 0:
            received = swapped(state_flat, "sx", bit_pos)
        else:
            received = swapped(state_flat, "sy", bit_pos)
        other_matrix = blocks(
            translate_re[level_no, own_bit, 1], translate_im[level_no, own_bit, 1]
        )
        total = own_part + jnp.dot(other_matrix, received, preferred_element_type=jnp.float32)
        product = base_product * (level_no + 1) % VGRID
        angles = (TWO_PI / VGRID * product.astype(jnp.float32)).reshape(columns)
        cosine = jnp.cos(angles)[None, :]
        sine_part = jnp.sin(angles)[None, :]
        real_total = total[:terms]
        imag_total = total[terms:]
        new_real = cosine * real_total - sine_part * imag_total
        new_imag = sine_part * real_total + cosine * imag_total
        state_flat = jnp.concatenate([new_real, new_imag], axis=0).astype(jnp.bfloat16)
    evaluate = jnp.concatenate([eval_re, -eval_im], axis=1)
    side = math.isqrt(eval_re.shape[0])
    picture = jnp.dot(evaluate, state_flat, preferred_element_type=jnp.float32).astype(jnp.bfloat16)
    picture = picture.reshape(side, side, columns)
    padded = with_halo(picture, (("sx", 0), ("sy", 1)), 2)
    values = padded.astype(jnp.float32)
    rows_near = values[1:-3] + values[2:-2] + values[3:-1]
    rows_far = rows_near + values[0:-4] + values[4:]
    box_near = rows_near[:, 1:-3] + rows_near[:, 2:-2] + rows_near[:, 3:-1]
    box_far = (
        rows_far[:, 1:-3]
        + rows_far[:, 2:-2]
        + rows_far[:, 3:-1]
        + rows_far[:, 0:-4]
        + rows_far[:, 4:]
    )
    chosen = jnp.where(window[0, 0] == 2, box_far / 25.0, box_near / 9.0)
    return chosen.astype(jnp.bfloat16)


MESH = pl.DeviceIdType.MESH
LANES = 128


def flipped(index, mask, total):
    bit = 1
    while bit < total:
        if mask & bit:
            index = index + bit - 2 * bit * (index // bit % 2)
        bit *= 2
    return index


def spread_kernel(
    nx,
    ny,
    src,
    extra,
    re_ref,
    im_ref,
    ere_ref,
    eim_ref,
    out,
    state,
    extras,
    mats,
    picture,
    tiles,
    rotors,
    send_sem,
    recv_sem,
    extra_send,
    extra_recv,
    out_send,
    out_recv,
):
    total_devices = nx * ny
    me = lax.axis_index("sx") * ny + lax.axis_index("sy")
    rows = src.shape[0]
    terms = rows // 2
    side = out.shape[0]
    columns = pl.ds(pl.multiple_of(me * LANES, LANES), LANES)

    barrier = pltpu.get_barrier_semaphore()

    @pl.loop(1, total_devices)
    def _(step):
        peer = lax.rem(me + step, total_devices)
        pl.semaphore_signal(
            barrier, inc=1, device_id=(peer // ny, lax.rem(peer, ny)), device_id_type=MESH
        )

    pl.semaphore_wait(barrier, total_devices - 1)

    half = ny // 2
    order = sorted(range(1, total_devices), key=lambda mask: (0 if mask & half else 1, mask))
    sends = []
    for mask in order:
        peer = flipped(me, mask, total_devices)
        where = (peer // ny, lax.rem(peer, ny))
        theirs = pl.ds(pl.multiple_of(peer * LANES, LANES), LANES)
        small = pltpu.make_async_remote_copy(
            src_ref=extra.at[peer],
            dst_ref=extras.at[me],
            send_sem=extra_send.at[mask],
            recv_sem=extra_recv.at[me],
            device_id=where,
            device_id_type=MESH,
        )
        large = pltpu.make_async_remote_copy(
            src_ref=src.at[:, theirs],
            dst_ref=state.at[me],
            send_sem=send_sem.at[mask],
            recv_sem=recv_sem.at[me],
            device_id=where,
            device_id_type=MESH,
        )
        small.start()
        large.start()
        sends += [small, large]
    pltpu.make_async_copy(extra.at[me], extras.at[me], extra_recv.at[me]).start()
    pltpu.make_async_copy(src.at[:, columns], state.at[me], recv_sem.at[me]).start()

    for level in range(LEVELS):
        for bit in range(2):
            for term in range(2):
                place = bit if term == 0 else 1 - bit
                top = bit * rows
                left = place * rows
                real = re_ref[level, bit, term]
                imag = im_ref[level, bit, term]
                mats[level, top : top + terms, left : left + terms] = real
                mats[level, top : top + terms, left + terms : left + rows] = -imag
                mats[level, top + terms : top + rows, left : left + terms] = imag
                mats[level, top + terms : top + rows, left + terms : left + rows] = real
    evaluate = jnp.concatenate([ere_ref[...], -eim_ref[...]], axis=1)
    picture[...] = jnp.zeros_like(picture)

    @pl.loop(0, total_devices)
    def _(box):
        pltpu.make_async_copy(extras.at[box], extras.at[box], extra_recv.at[box]).wait()
        cosine = extras[box, :, 0:LANES]
        sine = extras[box, :, LANES : 2 * LANES]
        real, imag = cosine, sine
        for level in range(LEVELS):
            rotors[level, 0, box] = real
            rotors[level, 1, box] = imag
            if level + 1 < LEVELS:
                real, imag = real * cosine - imag * sine, real * sine + imag * cosine

    def first_of(pair, stride):
        return pair // stride * (2 * stride) + lax.rem(pair, stride)

    for level in range(LEVELS):
        axis_size = nx if level % 2 == 0 else ny
        stride = (ny if level % 2 == 0 else 1) << (axis_size.bit_length() - 2 - level // 2)

        def advance(group, _, level=level, stride=stride):
            boxes = []
            for part in range(2):
                low = first_of(2 * group + part, stride)
                boxes.append((low, low + stride))
            if level == 0:
                for pair in boxes:
                    for box in pair:
                        pltpu.make_async_copy(state.at[box], state.at[box], recv_sem.at[box]).wait()
            stacked = jnp.concatenate(
                [jnp.concatenate([state[low], state[high]], axis=0) for low, high in boxes], axis=1
            )
            sums = jnp.dot(mats[level], stacked, preferred_element_type=jnp.float32)
            for part, pair in enumerate(boxes):
                for bit, box in enumerate(pair):
                    piece = sums[bit * rows : (bit + 1) * rows, part * LANES : (part + 1) * LANES]
                    real, imag = piece[:terms], piece[terms:]
                    cosine = rotors[level, 0, box]
                    sine = rotors[level, 1, box]
                    state[box, 0:terms] = (cosine * real - sine * imag).astype(jnp.bfloat16)
                    state[box, terms:rows] = (sine * real + cosine * imag).astype(jnp.bfloat16)
            return 0

        lax.fori_loop(0, total_devices // 4, advance, 0)

    def render(group, _):
        boxes = [2 * group, 2 * group + 1]
        stacked = jnp.concatenate([state[box] for box in boxes], axis=1)
        cells = jnp.dot(evaluate, stacked, preferred_element_type=jnp.float32)
        cells = cells.astype(jnp.bfloat16).astype(jnp.float32)
        for part, box in enumerate(boxes):
            block = cells[:, part * LANES : (part + 1) * LANES].reshape(side, side, LANES)
            picture[pl.ds(box // ny * side + 2, side), lax.rem(box, ny) + 1] = block
        return 0

    lax.fori_loop(0, total_devices // 2, render, 0)

    def smooth(box):
        row, col = box // ny, lax.rem(box, ny)
        values = picture[pl.ds(row * side, side + 4), pl.ds(col, 3)]
        rows_near = values[1:-3] + values[2:-2] + values[3:-1]
        rows_far = rows_near + values[0:-4] + values[4:]
        rows_near = rows_near.reshape(side, 3 * side, LANES)
        rows_far = rows_far.reshape(side, 3 * side, LANES)

        def moved(block, shift):
            return block[:, side + shift : 2 * side + shift]

        box_near = moved(rows_near, -1) + moved(rows_near, 0) + moved(rows_near, 1)
        box_far = (
            moved(rows_far, -1)
            + moved(rows_far, 0)
            + moved(rows_far, 1)
            + moved(rows_far, -2)
            + moved(rows_far, 2)
        )
        wide = extras[box, :, 2 * LANES : 3 * LANES].reshape(1, 1, LANES) == 2.0
        tiles[box] = jnp.where(wide, box_far / 25.0, box_near / 9.0).astype(jnp.bfloat16)

    for mask in order:
        peer = flipped(me, mask, total_devices)
        smooth(peer)
        done = pltpu.make_async_remote_copy(
            src_ref=tiles.at[peer],
            dst_ref=out.at[:, :, columns],
            send_sem=out_send.at[mask],
            recv_sem=out_recv.at[me],
            device_id=(peer // ny, lax.rem(peer, ny)),
            device_id_type=MESH,
        )
        done.start()
        sends.append(done)
    smooth(me)
    pltpu.make_async_copy(tiles.at[me], out.at[:, :, columns], out_recv.at[me]).start()

    for copy in sends:
        copy.wait_send()

    @pl.loop(0, total_devices)
    def _(box):
        pltpu.make_async_copy(tiles.at[box], tiles.at[box], out_recv.at[box]).wait()


def spread_on_device(
    nx,
    ny,
    sources,
    translate_re,
    translate_im,
    frame_index,
    velocity_index,
    eval_re,
    eval_im,
    window,
):
    total_devices = nx * ny
    terms, columns = sources.shape[3:]
    rows = 2 * terms
    side = math.isqrt(eval_re.shape[0])
    product = frame_index[0, 0][:, None] * velocity_index[0, 0][None, :] % VGRID
    angles = (TWO_PI / VGRID * product.astype(jnp.float32)).reshape(total_devices, 1, LANES)
    widths = jnp.broadcast_to(window[0, 0].astype(jnp.float32), angles.shape)
    extra = jnp.concatenate([jnp.cos(angles), jnp.sin(angles), widths], axis=-1)
    anywhere = pl.BlockSpec(memory_space=pl.ANY)
    inside = pl.BlockSpec(memory_space=pltpu.VMEM)
    dma = pltpu.SemaphoreType.DMA((total_devices,))
    return pl.pallas_call(
        functools.partial(spread_kernel, nx, ny),
        out_shape=jax.ShapeDtypeStruct((side, side, columns), jnp.bfloat16),
        in_specs=[anywhere, anywhere, inside, inside, inside, inside],
        out_specs=anywhere,
        scratch_shapes=[
            pltpu.VMEM((total_devices, rows, LANES), jnp.bfloat16),
            pltpu.VMEM((total_devices, 1, 3 * LANES), jnp.float32),
            pltpu.VMEM((LEVELS, 2 * rows, 2 * rows), jnp.bfloat16),
            pltpu.VMEM((nx * side + 4, ny + 2, side, LANES), jnp.float32),
            pltpu.VMEM((total_devices, side, side, LANES), jnp.bfloat16),
            pltpu.VMEM((LEVELS, 2, total_devices, 1, LANES), jnp.float32),
            dma,
            dma,
            dma,
            dma,
            dma,
            dma,
        ],
        compiler_params=pltpu.CompilerParams(collective_id=0, has_side_effects=True),
    )(
        sources[0, 0].reshape(rows, columns),
        extra,
        translate_re,
        translate_im,
        eval_re,
        eval_im,
    )


def solution(mesh):
    nx, ny = mesh.shape["sx"], mesh.shape["sy"]

    def body(sources, *others):
        share, left = divmod(sources.shape[4], nx * ny)
        if share == LANES and left == 0:
            return spread_on_device(nx, ny, sources, *others)
        return on_device(sources, *others)

    return jax.shard_map(
        body,
        mesh=mesh,
        in_specs=(
            P("sx", "sy", None, None, None),
            P(),
            P(),
            P("sx", "sy", None),
            P("sx", "sy", None),
            P(),
            P(),
            P("sx", "sy"),
        ),
        out_specs=P("sx", "sy", None),
        check_vma=False,
    )
```

```python
import functools
import math

import jax
import jax.numpy as jnp
from jax import lax
from jax.experimental import pallas as pl
from jax.experimental.pallas import tpu as pltpu
from jax.sharding import PartitionSpec as P

LEVELS = 4
VGRID = 4096


TWO_PI = 2.0 * math.pi


def swapped(block, axis, bit):
    count = lax.axis_size(axis)
    route = []
    for low in range(count):
        high = low | 1 << bit
        if high != low and high < count:
            route += [(low, high), (high, low)]
    return lax.ppermute(block, axis, route)


def with_halo(block, sides, width):
    for axis, dim in sides:
        count = lax.axis_size(axis)
        forward = [(i, i + 1) for i in range(count - 1)]
        backward = [(target, source) for source, target in forward]
        low = lax.ppermute(
            lax.slice_in_dim(block, block.shape[dim] - width, None, axis=dim), axis, forward
        )
        high = lax.ppermute(lax.slice_in_dim(block, 0, width, axis=dim), axis, backward)
        block = jnp.concatenate([low, block, high], axis=dim)
    return block


def blocks(real_part, imag_part):
    upper = jnp.concatenate([real_part, -imag_part], axis=-1)
    lower = jnp.concatenate([imag_part, real_part], axis=-1)
    return jnp.concatenate([upper, lower], axis=-2)


def on_device(
    sources, translate_re, translate_im, frame_index, velocity_index, eval_re, eval_im, window
):
    terms = sources.shape[3]
    columns = sources.shape[4]
    state_flat = sources[0, 0].reshape(2 * terms, columns)
    base_product = frame_index[0, 0][:, None] * velocity_index[0, 0][None, :]
    for level_no in range(LEVELS):
        if level_no % 2 == 0:
            bit_pos = lax.axis_size("sx").bit_length() - 2 - level_no // 2
            own_bit = lax.axis_index("sx") >> bit_pos & 1
        else:
            bit_pos = lax.axis_size("sy").bit_length() - 2 - level_no // 2
            own_bit = lax.axis_index("sy") >> bit_pos & 1
        self_matrix = blocks(translate_re[level_no, own_bit, 0], translate_im[level_no, own_bit, 0])
        own_part = jnp.dot(self_matrix, state_flat, preferred_element_type=jnp.float32)
        if level_no % 2 == 0:
            received = swapped(state_flat, "sx", bit_pos)
        else:
            received = swapped(state_flat, "sy", bit_pos)
        other_matrix = blocks(
            translate_re[level_no, own_bit, 1], translate_im[level_no, own_bit, 1]
        )
        total = own_part + jnp.dot(other_matrix, received, preferred_element_type=jnp.float32)
        product = base_product * (level_no + 1) % VGRID
        angles = (TWO_PI / VGRID * product.astype(jnp.float32)).reshape(columns)
        cosine = jnp.cos(angles)[None, :]
        sine_part = jnp.sin(angles)[None, :]
        real_total = total[:terms]
        imag_total = total[terms:]
        new_real = cosine * real_total - sine_part * imag_total
        new_imag = sine_part * real_total + cosine * imag_total
        state_flat = jnp.concatenate([new_real, new_imag], axis=0).astype(jnp.bfloat16)
    evaluate = jnp.concatenate([eval_re, -eval_im], axis=1)
    side = math.isqrt(eval_re.shape[0])
    picture = jnp.dot(evaluate, state_flat, preferred_element_type=jnp.float32).astype(jnp.bfloat16)
    picture = picture.reshape(side, side, columns)
    padded = with_halo(picture, (("sx", 0), ("sy", 1)), 2)
    values = padded.astype(jnp.float32)
    rows_near = values[1:-3] + values[2:-2] + values[3:-1]
    rows_far = rows_near + values[0:-4] + values[4:]
    box_near = rows_near[:, 1:-3] + rows_near[:, 2:-2] + rows_near[:, 3:-1]
    box_far = (
        rows_far[:, 1:-3]
        + rows_far[:, 2:-2]
        + rows_far[:, 3:-1]
        + rows_far[:, 0:-4]
        + rows_far[:, 4:]
    )
    chosen = jnp.where(window[0, 0] == 2, box_far / 25.0, box_near / 9.0)
    return chosen.astype(jnp.bfloat16)


MESH = pl.DeviceIdType.MESH
LANES = 128
UNROLL = 8


def flipped(index, mask, total):
    bit = 1
    while bit < total:
        if mask & bit:
            index = index + bit - 2 * bit * (index // bit % 2)
        bit *= 2
    return index


def spread_kernel(
    nx,
    ny,
    src,
    extra,
    re_hbm,
    im_hbm,
    ere_hbm,
    eim_hbm,
    out,
    state,
    partial,
    extras,
    mats,
    split_mats,
    picture,
    tiles,
    rotors,
    re_ref,
    im_ref,
    ere_ref,
    eim_ref,
    operand_sem,
    send_sem,
    recv_sem,
    extra_send,
    extra_recv,
    out_send,
    out_recv,
):
    total_devices = nx * ny
    depth = ny // 2
    members = nx * depth
    chunks = state.shape[0]
    my_x, my_y = lax.axis_index("sx"), lax.axis_index("sy")
    my_half = my_y // depth
    my_place = my_x * depth + lax.rem(my_y, depth)
    me = my_x * ny + my_y
    rows = src.shape[0]
    terms = rows // 2
    side = out.shape[1]

    def box_of(far, place):
        half = my_half + far - 2 * my_half * far
        return place // depth * ny + half * depth + lax.rem(place, depth)

    def coordinates(box):
        return box // ny, lax.rem(box, ny)

    def lanes_of(place, chunk):
        return pl.ds(pl.multiple_of((place * chunks + chunk) * LANES, LANES), LANES)

    barrier = pltpu.get_barrier_semaphore()

    @pl.loop(1, total_devices)
    def _(step):
        peer = lax.rem(me + step, total_devices)
        pl.semaphore_signal(barrier, inc=1, device_id=coordinates(peer), device_id_type=MESH)

    loads = [
        pltpu.make_async_copy(hbm, ref, operand_sem.at[number])
        for number, (hbm, ref) in enumerate(
            [(re_hbm, re_ref), (im_hbm, im_ref), (ere_hbm, ere_ref), (eim_hbm, eim_ref)]
        )
    ]
    for load in loads:
        load.start()
    for chunk in range(chunks):
        pltpu.make_async_copy(
            src.at[:, lanes_of(my_place, chunk)],
            state.at[chunk, my_place],
            recv_sem.at[chunk, my_place],
        ).start()
    pltpu.make_async_copy(extra.at[my_place], extras.at[me], extra_recv.at[me]).start()
    picture[...] = jnp.zeros_like(picture)

    pl.semaphore_wait(barrier, total_devices - 1)

    sends = []
    for chunk in range(chunks):
        for mask in range(1, members):
            place = flipped(my_place, mask, members)
            copy = pltpu.make_async_remote_copy(
                src_ref=src.at[:, lanes_of(place, chunk)],
                dst_ref=state.at[chunk, my_place],
                send_sem=send_sem.at[chunk, mask],
                recv_sem=recv_sem.at[chunk, my_place],
                device_id=coordinates(box_of(0, place)),
                device_id_type=MESH,
            )
            copy.start()
            sends.append(copy)
        if chunk:
            continue
        for far in range(2):
            for mask in range(1 - far, members):
                place = flipped(my_place, mask, members)
                copy = pltpu.make_async_remote_copy(
                    src_ref=extra.at[place],
                    dst_ref=extras.at[me],
                    send_sem=extra_send.at[far, mask],
                    recv_sem=extra_recv.at[me],
                    device_id=coordinates(box_of(far, place)),
                    device_id_type=MESH,
                )
                copy.start()
                sends.append(copy)

    for load in loads:
        load.wait()

    def put_matrix(target, top, left, level, bit, term):
        real = re_ref[level, bit, term]
        imag = im_ref[level, bit, term]
        target[top : top + terms, left : left + terms] = real
        target[top : top + terms, left + terms : left + rows] = -imag
        target[top + terms : top + rows, left : left + terms] = imag
        target[top + terms : top + rows, left + terms : left + rows] = real

    for level in range(LEVELS):
        if level == 1:
            put_matrix(split_mats, 0, 0, level, my_half, 0)
            put_matrix(split_mats, rows, 0, level, 1 - my_half, 1)
            continue
        for bit in range(2):
            put_matrix(mats.at[level], bit * rows, bit * rows, level, bit, 0)
            put_matrix(mats.at[level], bit * rows, (1 - bit) * rows, level, bit, 1)
    evaluate = jnp.concatenate([ere_ref[...], -eim_ref[...]], axis=1)

    @pl.loop(0, total_devices)
    def _(box):
        pltpu.make_async_copy(extras.at[box], extras.at[box], extra_recv.at[box]).wait()
        for chunk in range(chunks):
            cosine = extras[box, :, chunk * LANES : (chunk + 1) * LANES]
            sine = extras[box, :, (chunks + chunk) * LANES : (chunks + chunk + 1) * LANES]
            real, imag = cosine, sine
            for level in range(LEVELS):
                rotors[chunk, level, 0, box] = real
                rotors[chunk, level, 1, box] = imag
                if level + 1 < LEVELS:
                    real, imag = real * cosine - imag * sine, real * sine + imag * cosine

    def turned(piece, chunk, level, box):
        real, imag = piece[:terms], piece[terms:]
        cosine = rotors[chunk, level, 0, box]
        sine = rotors[chunk, level, 1, box]
        new_real = (cosine * real - sine * imag).astype(jnp.bfloat16)
        new_imag = (sine * real + cosine * imag).astype(jnp.bfloat16)
        return new_real, new_imag

    def pairs_of(group, level):
        axis_size = nx if level % 2 == 0 else ny
        stride = (depth if level % 2 == 0 else 1) << (axis_size.bit_length() - 2 - level // 2)
        found = []
        for part in range(2):
            pair = 2 * group + part
            low = pair // stride * (2 * stride) + lax.rem(pair, stride)
            found.append((low, low + stride))
        return found

    def exchange(boxes_ref, chunk, level, far, group):
        pairs = pairs_of(group, level)
        stacked = jnp.concatenate(
            [jnp.concatenate([boxes_ref[low], boxes_ref[high]], axis=0) for low, high in pairs],
            axis=1,
        )
        sums = jnp.dot(mats[level], stacked, preferred_element_type=jnp.float32)
        for part, pair in enumerate(pairs):
            for bit, place in enumerate(pair):
                piece = sums[bit * rows : (bit + 1) * rows, part * LANES : (part + 1) * LANES]
                real, imag = turned(piece, chunk, level, box_of(far, place))
                boxes_ref[place, 0:terms] = real
                boxes_ref[place, terms:rows] = imag

    @pl.loop(0, chunks)
    def _(chunk):
        @pl.loop(0, members)
        def _(place):
            block = state.at[chunk, place]
            pltpu.make_async_copy(block, block, recv_sem.at[chunk, place]).wait()

        def first(group, _):
            exchange(state.at[chunk], chunk, 0, 0, group)
            return 0

        lax.fori_loop(0, members // 4, first, 0, unroll=UNROLL)

        def second(group, _):
            places = [2 * group, 2 * group + 1]
            stacked = jnp.concatenate([state[chunk, place] for place in places], axis=1)
            sums = jnp.dot(split_mats[...], stacked, preferred_element_type=jnp.float32)
            for part, place in enumerate(places):
                for far in range(2):
                    piece = sums[far * rows : (far + 1) * rows, part * LANES : (part + 1) * LANES]
                    real, imag = turned(piece, chunk, 1, box_of(far, place))
                    partial[far, place, 0:terms] = real
                    partial[far, place, terms:rows] = imag
            return 0

        lax.fori_loop(0, members // 2, second, 0, unroll=UNROLL)

        for level in range(2, LEVELS):

            def later(step, _, level=level):
                for far in range(2):
                    exchange(partial.at[far], chunk, level, far, step)
                return 0

            lax.fori_loop(0, members // 4, later, 0, unroll=UNROLL)

        def render(place, _):
            stacked = jnp.concatenate([partial[0, place], partial[1, place]], axis=1)
            cells = jnp.dot(evaluate, stacked, preferred_element_type=jnp.float32)
            for far in range(2):
                block = cells[:, far * LANES : (far + 1) * LANES].reshape(side, side, LANES)
                row, col = coordinates(box_of(far, place))
                picture[pl.ds(row * side + 2, side), col + 1] = block
            return 0

        lax.fori_loop(0, members, render, 0, unroll=UNROLL)

        def smooth(far, place):
            box = box_of(far, place)
            row, col = coordinates(box)
            values = picture[pl.ds(row * side, side + 4), pl.ds(col, 3)]
            rows_near = values[1:-3] + values[2:-2] + values[3:-1]
            rows_far = rows_near + values[0:-4] + values[4:]
            rows_near = rows_near.reshape(side, 3 * side, LANES)
            rows_far = rows_far.reshape(side, 3 * side, LANES)

            def moved(block, shift):
                return block[:, side + shift : 2 * side + shift]

            box_near = moved(rows_near, -1) + moved(rows_near, 0) + moved(rows_near, 1)
            box_far = (
                moved(rows_far, -1)
                + moved(rows_far, 0)
                + moved(rows_far, 1)
                + moved(rows_far, -2)
                + moved(rows_far, 2)
            )
            wide = extras[box, :, 2 * chunks * LANES :].reshape(1, 1, LANES) == 2.0
            chosen = jnp.where(wide, box_far / 25.0, box_near / 9.0)
            tiles[chunk, far, place] = chosen.astype(jnp.bfloat16)

        for far in (1, 0):
            for mask in range(members):
                place = flipped(my_place, mask, members)
                smooth(far, place)
                source = tiles.at[chunk, far, place]
                target = out.at[far, :, :, lanes_of(my_place, chunk)]
                arrived = out_recv.at[chunk, far, my_place]
                if far == 0 and mask == 0:
                    pltpu.make_async_copy(source, target, arrived).start()
                else:
                    pltpu.make_async_remote_copy(
                        src_ref=source,
                        dst_ref=target,
                        send_sem=out_send.at[chunk, far, mask],
                        recv_sem=arrived,
                        device_id=coordinates(box_of(far, place)),
                        device_id_type=MESH,
                    ).start()

    for copy in sends:
        copy.wait_send()

    for far in range(2):
        for chunk in range(chunks):

            @pl.loop(1 - far, members)
            def _(mask, far=far, chunk=chunk):
                block = tiles.at[chunk, far, mask]
                pltpu.make_async_copy(block, block, out_send.at[chunk, far, mask]).wait()

            @pl.loop(0, members)
            def _(place, far=far, chunk=chunk):
                block = tiles.at[chunk, far, place]
                pltpu.make_async_copy(block, block, out_recv.at[chunk, far, place]).wait()


def spread_on_device(
    nx,
    ny,
    sources,
    translate_re,
    translate_im,
    frame_index,
    velocity_index,
    eval_re,
    eval_im,
    window,
):
    total_devices = nx * ny
    members = total_devices // 2
    terms, columns = sources.shape[3:]
    rows = 2 * terms
    side = math.isqrt(eval_re.shape[0])
    share = columns // members
    chunks = share // LANES
    product = frame_index[0, 0][:, None] * velocity_index[0, 0][None, :] % VGRID
    angles = (TWO_PI / VGRID * product.astype(jnp.float32)).reshape(members, 1, share)
    widths = jnp.broadcast_to(window[0, 0].astype(jnp.float32), (members, 1, LANES))
    extra = jnp.concatenate([jnp.cos(angles), jnp.sin(angles), widths], axis=-1)
    anywhere = pl.BlockSpec(memory_space=pl.ANY)
    dma = pltpu.SemaphoreType.DMA
    halves = pl.pallas_call(
        functools.partial(spread_kernel, nx, ny),
        out_shape=jax.ShapeDtypeStruct((2, side, side, columns), jnp.bfloat16),
        in_specs=[anywhere] * 6,
        out_specs=anywhere,
        scratch_shapes=[
            pltpu.VMEM((chunks, members, rows, LANES), jnp.bfloat16),
            pltpu.VMEM((2, members, rows, LANES), jnp.bfloat16),
            pltpu.VMEM((total_devices, 1, 2 * share + LANES), jnp.float32),
            pltpu.VMEM((LEVELS, 2 * rows, 2 * rows), jnp.bfloat16),
            pltpu.VMEM((2 * rows, rows), jnp.bfloat16),
            pltpu.VMEM((nx * side + 4, ny + 2, side, LANES), jnp.float32),
            pltpu.VMEM((chunks, 2, members, side, side, LANES), jnp.bfloat16),
            pltpu.VMEM((chunks, LEVELS, 2, total_devices, 1, LANES), jnp.float32),
            pltpu.VMEM(translate_re.shape, jnp.bfloat16),
            pltpu.VMEM(translate_im.shape, jnp.bfloat16),
            pltpu.VMEM(eval_re.shape, jnp.bfloat16),
            pltpu.VMEM(eval_im.shape, jnp.bfloat16),
            dma((4,)),
            dma((chunks, members)),
            dma((chunks, members)),
            dma((2, members)),
            dma((total_devices,)),
            dma((chunks, 2, members)),
            dma((chunks, 2, members)),
        ],
        compiler_params=pltpu.CompilerParams(collective_id=0, has_side_effects=True),
    )(
        sources[0, 0].reshape(rows, columns),
        extra,
        translate_re,
        translate_im,
        eval_re,
        eval_im,
    )
    return (halves[0].astype(jnp.float32) + halves[1].astype(jnp.float32)).astype(jnp.bfloat16)


def solution(mesh):
    nx, ny = mesh.shape["sx"], mesh.shape["sy"]

    def body(sources, *others):
        members = nx * ny // 2
        if sources.shape[4] % (members * LANES) == 0:
            return spread_on_device(nx, ny, sources, *others)
        return on_device(sources, *others)

    return jax.shard_map(
        body,
        mesh=mesh,
        in_specs=(
            P("sx", "sy", None, None, None),
            P(),
            P(),
            P("sx", "sy", None),
            P("sx", "sy", None),
            P(),
            P(),
            P("sx", "sy"),
        ),
        out_specs=P("sx", "sy", None),
        check_vma=False,
    )
```

```python
import functools
import math

import jax
import jax.numpy as jnp
from jax import lax
from jax.experimental import pallas as pl
from jax.experimental.pallas import tpu as pltpu
from jax.sharding import PartitionSpec as P

LEVELS = 4
VGRID = 4096


TWO_PI = 2.0 * math.pi


def swapped(block, axis, bit):
    count = lax.axis_size(axis)
    route = []
    for low in range(count):
        high = low | 1 << bit
        if high != low and high < count:
            route += [(low, high), (high, low)]
    return lax.ppermute(block, axis, route)


def with_halo(block, sides, width):
    for axis, dim in sides:
        count = lax.axis_size(axis)
        forward = [(i, i + 1) for i in range(count - 1)]
        backward = [(target, source) for source, target in forward]
        low = lax.ppermute(
            lax.slice_in_dim(block, block.shape[dim] - width, None, axis=dim), axis, forward
        )
        high = lax.ppermute(lax.slice_in_dim(block, 0, width, axis=dim), axis, backward)
        block = jnp.concatenate([low, block, high], axis=dim)
    return block


def blocks(real_part, imag_part):
    upper = jnp.concatenate([real_part, -imag_part], axis=-1)
    lower = jnp.concatenate([imag_part, real_part], axis=-1)
    return jnp.concatenate([upper, lower], axis=-2)


def on_device(
    sources, translate_re, translate_im, frame_index, velocity_index, eval_re, eval_im, window
):
    terms = sources.shape[3]
    columns = sources.shape[4]
    state_flat = sources[0, 0].reshape(2 * terms, columns)
    base_product = frame_index[0, 0][:, None] * velocity_index[0, 0][None, :]
    for level_no in range(LEVELS):
        if level_no % 2 == 0:
            bit_pos = lax.axis_size("sx").bit_length() - 2 - level_no // 2
            own_bit = lax.axis_index("sx") >> bit_pos & 1
        else:
            bit_pos = lax.axis_size("sy").bit_length() - 2 - level_no // 2
            own_bit = lax.axis_index("sy") >> bit_pos & 1
        self_matrix = blocks(translate_re[level_no, own_bit, 0], translate_im[level_no, own_bit, 0])
        own_part = jnp.dot(self_matrix, state_flat, preferred_element_type=jnp.float32)
        if level_no % 2 == 0:
            received = swapped(state_flat, "sx", bit_pos)
        else:
            received = swapped(state_flat, "sy", bit_pos)
        other_matrix = blocks(
            translate_re[level_no, own_bit, 1], translate_im[level_no, own_bit, 1]
        )
        total = own_part + jnp.dot(other_matrix, received, preferred_element_type=jnp.float32)
        product = base_product * (level_no + 1) % VGRID
        angles = (TWO_PI / VGRID * product.astype(jnp.float32)).reshape(columns)
        cosine = jnp.cos(angles)[None, :]
        sine_part = jnp.sin(angles)[None, :]
        real_total = total[:terms]
        imag_total = total[terms:]
        new_real = cosine * real_total - sine_part * imag_total
        new_imag = sine_part * real_total + cosine * imag_total
        state_flat = jnp.concatenate([new_real, new_imag], axis=0).astype(jnp.bfloat16)
    evaluate = jnp.concatenate([eval_re, -eval_im], axis=1)
    side = math.isqrt(eval_re.shape[0])
    picture = jnp.dot(evaluate, state_flat, preferred_element_type=jnp.float32).astype(jnp.bfloat16)
    picture = picture.reshape(side, side, columns)
    padded = with_halo(picture, (("sx", 0), ("sy", 1)), 2)
    values = padded.astype(jnp.float32)
    rows_near = values[1:-3] + values[2:-2] + values[3:-1]
    rows_far = rows_near + values[0:-4] + values[4:]
    box_near = rows_near[:, 1:-3] + rows_near[:, 2:-2] + rows_near[:, 3:-1]
    box_far = (
        rows_far[:, 1:-3]
        + rows_far[:, 2:-2]
        + rows_far[:, 3:-1]
        + rows_far[:, 0:-4]
        + rows_far[:, 4:]
    )
    chosen = jnp.where(window[0, 0] == 2, box_far / 25.0, box_near / 9.0)
    return chosen.astype(jnp.bfloat16)


MESH = pl.DeviceIdType.MESH
LANES = 128
UNROLL = 4


def flipped(index, mask, total):
    bit = 1
    while bit < total:
        if mask & bit:
            index = index + bit - 2 * bit * (index // bit % 2)
        bit *= 2
    return index


def spread_kernel(
    nx,
    ny,
    src,
    extra,
    re_hbm,
    im_hbm,
    ere_hbm,
    eim_hbm,
    out,
    other,
    state,
    whole,
    partial,
    extras,
    mats,
    split_mats,
    picture,
    tiles,
    whole_tiles,
    rotors,
    re_ref,
    im_ref,
    ere_ref,
    eim_ref,
    operand_sem,
    send_sem,
    recv_sem,
    whole_send,
    whole_recv,
    extra_send,
    extra_recv,
    out_send,
    out_recv,
    whole_out_send,
    whole_out_recv,
):
    total_devices = nx * ny
    depth = ny // 2
    members = nx * depth
    my_x, my_y = lax.axis_index("sx"), lax.axis_index("sy")
    my_half = my_y // depth
    my_place = my_x * depth + lax.rem(my_y, depth)
    me = my_x * ny + my_y
    my_seat = my_x // 2 * ny + my_y
    seated = lax.rem(my_x, 2) == 0
    rows = src.shape[0]
    terms = rows // 2
    side = out.shape[0]

    def box_of(far, place):
        half = my_half + far - 2 * my_half * far
        return place // depth * ny + half * depth + lax.rem(place, depth)

    def coordinates(box):
        return box // ny, lax.rem(box, ny)

    def box_at(seat):
        return seat // ny * 2 * ny + lax.rem(seat, ny)

    def lanes_of(number):
        return pl.ds(pl.multiple_of(number * LANES, LANES), LANES)

    barrier = pltpu.get_barrier_semaphore()

    @pl.loop(1, total_devices)
    def _(step):
        peer = lax.rem(me + step, total_devices)
        pl.semaphore_signal(barrier, inc=1, device_id=coordinates(peer), device_id_type=MESH)

    loads = [
        pltpu.make_async_copy(hbm, ref, operand_sem.at[number])
        for number, (hbm, ref) in enumerate(
            [(re_hbm, re_ref), (im_hbm, im_ref), (ere_hbm, ere_ref), (eim_hbm, eim_ref)]
        )
    ]
    for load in loads:
        load.start()
    pltpu.make_async_copy(
        src.at[:, lanes_of(my_place)], state.at[my_place], recv_sem.at[my_place]
    ).start()
    pltpu.make_async_copy(extra.at[my_place], extras.at[0, me], extra_recv.at[0, me]).start()

    @pl.when(seated)
    def _():
        number = members + my_seat
        pltpu.make_async_copy(
            src.at[:, lanes_of(number)], whole.at[me], whole_recv.at[me]
        ).start()
        pltpu.make_async_copy(extra.at[number], extras.at[1, me], extra_recv.at[1, me]).start()

    picture[...] = jnp.zeros_like(picture)

    pl.semaphore_wait(barrier, total_devices - 1)

    def send(source, target, sent, arrived, box):
        copy = pltpu.make_async_remote_copy(
            src_ref=source,
            dst_ref=target,
            send_sem=sent,
            recv_sem=arrived,
            device_id=coordinates(box),
            device_id_type=MESH,
        )
        copy.start()
        return copy

    sends = []
    for mask in range(1, members):
        place = flipped(my_place, mask, members)
        sends.append(
            send(
                src.at[:, lanes_of(place)],
                state.at[my_place],
                send_sem.at[mask],
                recv_sem.at[my_place],
                box_of(0, place),
            )
        )
    for far in range(2):
        for mask in range(1 - far, members):
            place = flipped(my_place, mask, members)
            sends.append(
                send(
                    extra.at[place],
                    extras.at[0, me],
                    extra_send.at[far, mask],
                    extra_recv.at[0, me],
                    box_of(far, place),
                )
            )

    def send_whole(mask):
        seat = flipped(my_seat, mask, members)
        number = members + seat
        return [
            send(
                src.at[:, lanes_of(number)],
                whole.at[me],
                whole_send.at[mask],
                whole_recv.at[me],
                box_at(seat),
            ),
            send(
                extra.at[number],
                extras.at[1, me],
                extra_send.at[2, mask],
                extra_recv.at[1, me],
                box_at(seat),
            ),
        ]

    half_mask = ny // 2
    for mask in sorted(range(1, members), key=lambda mask: (0 if mask & half_mask else 1, mask)):
        sends += send_whole(mask)

    @pl.when(jnp.logical_not(seated))
    def _():
        for copy in send_whole(0):
            copy.wait_send()

    for load in loads:
        load.wait()

    def put_matrix(target, top, left, level, bit, term):
        real = re_ref[level, bit, term]
        imag = im_ref[level, bit, term]
        target[top : top + terms, left : left + terms] = real
        target[top : top + terms, left + terms : left + rows] = -imag
        target[top + terms : top + rows, left : left + terms] = imag
        target[top + terms : top + rows, left + terms : left + rows] = real

    for level in range(LEVELS):
        if level == 1:
            put_matrix(split_mats, 0, 0, level, my_half, 0)
            put_matrix(split_mats, rows, 0, level, 1 - my_half, 1)
        for bit in range(2):
            put_matrix(mats.at[level], bit * rows, bit * rows, level, bit, 0)
            put_matrix(mats.at[level], bit * rows, (1 - bit) * rows, level, bit, 1)
    evaluate = jnp.concatenate([ere_ref[...], -eim_ref[...]], axis=1)

    def collect_rotors(kind):
        @pl.loop(0, total_devices)
        def _(box):
            block = extras.at[kind, box]
            pltpu.make_async_copy(block, block, extra_recv.at[kind, box]).wait()
            cosine = extras[kind, box, :, 0:LANES]
            sine = extras[kind, box, :, LANES : 2 * LANES]
            real, imag = cosine, sine
            for level in range(LEVELS):
                rotors[kind, level, 0, box] = real
                rotors[kind, level, 1, box] = imag
                if level + 1 < LEVELS:
                    real, imag = real * cosine - imag * sine, real * sine + imag * cosine

    def turned(piece, chunk, level, box):
        real, imag = piece[:terms], piece[terms:]
        cosine = rotors[chunk, level, 0, box]
        sine = rotors[chunk, level, 1, box]
        new_real = (cosine * real - sine * imag).astype(jnp.bfloat16)
        new_imag = (sine * real + cosine * imag).astype(jnp.bfloat16)
        return new_real, new_imag

    def exchange(boxes_ref, kind, level, box_at_index, width, group):
        axis_size = nx if level % 2 == 0 else ny
        stride = (width if level % 2 == 0 else 1) << (axis_size.bit_length() - 2 - level // 2)
        pairs = []
        for part in range(2):
            pair = 2 * group + part
            low = pair // stride * (2 * stride) + lax.rem(pair, stride)
            pairs.append((low, low + stride))
        stacked = jnp.concatenate(
            [jnp.concatenate([boxes_ref[low], boxes_ref[high]], axis=0) for low, high in pairs],
            axis=1,
        )
        sums = jnp.dot(mats[level], stacked, preferred_element_type=jnp.float32)
        for part, pair in enumerate(pairs):
            for bit, index in enumerate(pair):
                piece = sums[bit * rows : (bit + 1) * rows, part * LANES : (part + 1) * LANES]
                real, imag = turned(piece, kind, level, box_at_index(index))
                boxes_ref[index, 0:terms] = real
                boxes_ref[index, terms:rows] = imag

    def render(states, boxes):
        stacked = jnp.concatenate(states, axis=1)
        cells = jnp.dot(evaluate, stacked, preferred_element_type=jnp.float32)
        for part, box in enumerate(boxes):
            block = cells[:, part * LANES : (part + 1) * LANES].reshape(side, side, LANES)
            row, col = coordinates(box)
            picture[pl.ds(row * side + 2, side), col + 1] = block

    def smooth(box):
        row, col = coordinates(box)
        values = picture[pl.ds(row * side, side + 4), pl.ds(col, 3)]
        rows_near = values[1:-3] + values[2:-2] + values[3:-1]
        rows_far = rows_near + values[0:-4] + values[4:]
        rows_near = rows_near.reshape(side, 3 * side, LANES)
        rows_far = rows_far.reshape(side, 3 * side, LANES)

        def moved(block, shift):
            return block[:, side + shift : 2 * side + shift]

        box_near = moved(rows_near, -1) + moved(rows_near, 0) + moved(rows_near, 1)
        box_far = (
            moved(rows_far, -1)
            + moved(rows_far, 0)
            + moved(rows_far, 1)
            + moved(rows_far, -2)
            + moved(rows_far, 2)
        )
        wide = extras[0, box, :, 2 * LANES :].reshape(1, 1, LANES) == 2.0
        return jnp.where(wide, box_far / 25.0, box_near / 9.0).astype(jnp.bfloat16)

    def repeat(count, step):
        def body(index, _):
            step(index)
            return 0

        lax.fori_loop(0, count, body, 0, unroll=UNROLL)

    collect_rotors(0)

    @pl.loop(0, members)
    def _(place):
        block = state.at[place]
        pltpu.make_async_copy(block, block, recv_sem.at[place]).wait()

    repeat(
        members // 4, lambda group: exchange(state, 0, 0, lambda i: box_of(0, i), depth, group)
    )

    def split(group):
        places = [2 * group, 2 * group + 1]
        stacked = jnp.concatenate([state[place] for place in places], axis=1)
        sums = jnp.dot(split_mats[...], stacked, preferred_element_type=jnp.float32)
        for part, place in enumerate(places):
            for far in range(2):
                piece = sums[far * rows : (far + 1) * rows, part * LANES : (part + 1) * LANES]
                real, imag = turned(piece, 0, 1, box_of(far, place))
                partial[far, place, 0:terms] = real
                partial[far, place, terms:rows] = imag

    repeat(members // 2, split)
    for level in range(2, LEVELS):

        def later(group, level=level):
            for far in range(2):
                exchange(partial.at[far], 0, level, lambda i: box_of(far, i), depth, group)

        repeat(members // 4, later)
    repeat(
        members,
        lambda place: render(
            [partial[0, place], partial[1, place]], [box_of(0, place), box_of(1, place)]
        ),
    )
    for far in (1, 0):
        target = (other if far else out).at[:, :, lanes_of(my_place)]
        arrived = out_recv.at[far, my_place]
        for mask in range(members):
            place = flipped(my_place, mask, members)
            source = tiles.at[far, place]
            tiles[far, place] = smooth(box_of(far, place))
            if far == 0 and mask == 0:
                pltpu.make_async_copy(source, target, arrived).start()
            else:
                sent = out_send.at[far, mask]
                sends.append(send(source, target, sent, arrived, box_of(far, place)))

    @pl.when(seated)
    def _():
        collect_rotors(1)

        @pl.loop(0, total_devices)
        def _(box):
            block = whole.at[box]
            pltpu.make_async_copy(block, block, whole_recv.at[box]).wait()

        for level in range(LEVELS):
            repeat(
                total_devices // 4,
                lambda group, level=level: exchange(whole, 1, level, lambda i: i, ny, group),
            )
        repeat(
            total_devices // 2,
            lambda group: render(
                [whole[2 * group], whole[2 * group + 1]], [2 * group, 2 * group + 1]
            ),
        )
        target = out.at[:, :, lanes_of(members + my_seat)]
        arrived = whole_out_recv.at[my_seat]
        finals = []
        order = sorted(
            range(1, total_devices), key=lambda mask: (0 if mask & half_mask else 1, mask)
        )
        for mask in order:
            box = flipped(me, mask, total_devices)
            whole_tiles[box] = smooth(box).astype(jnp.bfloat16)
            sent = whole_out_send.at[mask]
            finals.append(send(whole_tiles.at[box], target, sent, arrived, box))
        whole_tiles[me] = smooth(me)
        pltpu.make_async_copy(whole_tiles.at[me], target, arrived).start()
        for copy in finals:
            copy.wait_send()

    for copy in sends:
        copy.wait_send()

    @pl.loop(0, members)
    def _(place):
        for far in range(2):
            block = tiles.at[far, place]
            pltpu.make_async_copy(block, block, out_recv.at[far, place]).wait()
        block = whole_tiles.at[place]
        pltpu.make_async_copy(block, block, whole_out_recv.at[place]).wait()


def spread_on_device(
    nx,
    ny,
    sources,
    translate_re,
    translate_im,
    frame_index,
    velocity_index,
    eval_re,
    eval_im,
    window,
):
    total_devices = nx * ny
    members = total_devices // 2
    terms, columns = sources.shape[3:]
    rows = 2 * terms
    side = math.isqrt(eval_re.shape[0])
    slabs = columns // LANES
    product = frame_index[0, 0][:, None] * velocity_index[0, 0][None, :] % VGRID
    angles = (TWO_PI / VGRID * product.astype(jnp.float32)).reshape(slabs, 1, LANES)
    widths = jnp.broadcast_to(window[0, 0].astype(jnp.float32), angles.shape)
    extra = jnp.concatenate([jnp.cos(angles), jnp.sin(angles), widths], axis=-1)
    anywhere = pl.BlockSpec(memory_space=pl.ANY)
    dma = pltpu.SemaphoreType.DMA
    vmem = pltpu.VMEM
    out, other = pl.pallas_call(
        functools.partial(spread_kernel, nx, ny),
        out_shape=(
            jax.ShapeDtypeStruct((side, side, columns), jnp.bfloat16),
            jax.ShapeDtypeStruct((side, side, members * LANES), jnp.bfloat16),
        ),
        in_specs=[anywhere] * 6,
        out_specs=(anywhere, anywhere),
        scratch_shapes=[
            vmem((members, rows, LANES), jnp.bfloat16),
            vmem((total_devices, rows, LANES), jnp.bfloat16),
            vmem((2, members, rows, LANES), jnp.bfloat16),
            vmem((2, total_devices, 1, 3 * LANES), jnp.float32),
            vmem((LEVELS, 2 * rows, 2 * rows), jnp.bfloat16),
            vmem((2 * rows, rows), jnp.bfloat16),
            vmem((nx * side + 4, ny + 2, side, LANES), jnp.float32),
            vmem((2, members, side, side, LANES), jnp.bfloat16),
            vmem((total_devices, side, side, LANES), jnp.bfloat16),
            vmem((2, LEVELS, 2, total_devices, 1, LANES), jnp.float32),
            vmem(translate_re.shape, jnp.bfloat16),
            vmem(translate_im.shape, jnp.bfloat16),
            vmem(eval_re.shape, jnp.bfloat16),
            vmem(eval_im.shape, jnp.bfloat16),
            dma((4,)),
            dma((members,)),
            dma((members,)),
            dma((members,)),
            dma((total_devices,)),
            dma((3, members)),
            dma((2, total_devices)),
            dma((2, members)),
            dma((2, members)),
            dma((total_devices,)),
            dma((members,)),
        ],
        compiler_params=pltpu.CompilerParams(collective_id=0, has_side_effects=True),
    )(
        sources[0, 0].reshape(rows, columns),
        extra,
        translate_re,
        translate_im,
        eval_re,
        eval_im,
    )
    other = jnp.pad(other, ((0, 0), (0, 0), (0, columns - other.shape[2])))
    return (out.astype(jnp.float32) + other.astype(jnp.float32)).astype(jnp.bfloat16)


def solution(mesh):
    nx, ny = mesh.shape["sx"], mesh.shape["sy"]

    def body(sources, *others):
        if sources.shape[4] == nx * ny * LANES:
            return spread_on_device(nx, ny, sources, *others)
        return on_device(sources, *others)

    return jax.shard_map(
        body,
        mesh=mesh,
        in_specs=(
            P("sx", "sy", None, None, None),
            P(),
            P(),
            P("sx", "sy", None),
            P("sx", "sy", None),
            P(),
            P(),
            P("sx", "sy"),
        ),
        out_specs=P("sx", "sy", None),
        check_vma=False,
    )
```

```python
import functools
import math

import jax
import jax.numpy as jnp
from jax import lax
from jax.experimental import pallas as pl
from jax.experimental.pallas import tpu as pltpu
from jax.sharding import PartitionSpec as P

LEVELS = 4
VGRID = 4096


TWO_PI = 2.0 * math.pi


def swapped(block, axis, bit):
    count = lax.axis_size(axis)
    route = []
    for low in range(count):
        high = low | 1 << bit
        if high != low and high < count:
            route += [(low, high), (high, low)]
    return lax.ppermute(block, axis, route)


def with_halo(block, sides, width):
    for axis, dim in sides:
        count = lax.axis_size(axis)
        forward = [(i, i + 1) for i in range(count - 1)]
        backward = [(target, source) for source, target in forward]
        low = lax.ppermute(
            lax.slice_in_dim(block, block.shape[dim] - width, None, axis=dim), axis, forward
        )
        high = lax.ppermute(lax.slice_in_dim(block, 0, width, axis=dim), axis, backward)
        block = jnp.concatenate([low, block, high], axis=dim)
    return block


def blocks(real_part, imag_part):
    upper = jnp.concatenate([real_part, -imag_part], axis=-1)
    lower = jnp.concatenate([imag_part, real_part], axis=-1)
    return jnp.concatenate([upper, lower], axis=-2)


def on_device(
    sources, translate_re, translate_im, frame_index, velocity_index, eval_re, eval_im, window
):
    terms = sources.shape[3]
    columns = sources.shape[4]
    state_flat = sources[0, 0].reshape(2 * terms, columns)
    base_product = frame_index[0, 0][:, None] * velocity_index[0, 0][None, :]
    for level_no in range(LEVELS):
        if level_no % 2 == 0:
            bit_pos = lax.axis_size("sx").bit_length() - 2 - level_no // 2
            own_bit = lax.axis_index("sx") >> bit_pos & 1
        else:
            bit_pos = lax.axis_size("sy").bit_length() - 2 - level_no // 2
            own_bit = lax.axis_index("sy") >> bit_pos & 1
        self_matrix = blocks(translate_re[level_no, own_bit, 0], translate_im[level_no, own_bit, 0])
        own_part = jnp.dot(self_matrix, state_flat, preferred_element_type=jnp.float32)
        if level_no % 2 == 0:
            received = swapped(state_flat, "sx", bit_pos)
        else:
            received = swapped(state_flat, "sy", bit_pos)
        other_matrix = blocks(
            translate_re[level_no, own_bit, 1], translate_im[level_no, own_bit, 1]
        )
        total = own_part + jnp.dot(other_matrix, received, preferred_element_type=jnp.float32)
        product = base_product * (level_no + 1) % VGRID
        angles = (TWO_PI / VGRID * product.astype(jnp.float32)).reshape(columns)
        cosine = jnp.cos(angles)[None, :]
        sine_part = jnp.sin(angles)[None, :]
        real_total = total[:terms]
        imag_total = total[terms:]
        new_real = cosine * real_total - sine_part * imag_total
        new_imag = sine_part * real_total + cosine * imag_total
        state_flat = jnp.concatenate([new_real, new_imag], axis=0).astype(jnp.bfloat16)
    evaluate = jnp.concatenate([eval_re, -eval_im], axis=1)
    side = math.isqrt(eval_re.shape[0])
    picture = jnp.dot(evaluate, state_flat, preferred_element_type=jnp.float32).astype(jnp.bfloat16)
    picture = picture.reshape(side, side, columns)
    padded = with_halo(picture, (("sx", 0), ("sy", 1)), 2)
    values = padded.astype(jnp.float32)
    rows_near = values[1:-3] + values[2:-2] + values[3:-1]
    rows_far = rows_near + values[0:-4] + values[4:]
    box_near = rows_near[:, 1:-3] + rows_near[:, 2:-2] + rows_near[:, 3:-1]
    box_far = (
        rows_far[:, 1:-3]
        + rows_far[:, 2:-2]
        + rows_far[:, 3:-1]
        + rows_far[:, 0:-4]
        + rows_far[:, 4:]
    )
    chosen = jnp.where(window[0, 0] == 2, box_far / 25.0, box_near / 9.0)
    return chosen.astype(jnp.bfloat16)


MESH = pl.DeviceIdType.MESH
LANES = 128
UNROLL = 4


def flipped(index, mask, total):
    bit = 1
    while bit < total:
        if mask & bit:
            index = index + bit - 2 * bit * (index // bit % 2)
        bit *= 2
    return index


def spread_kernel(
    nx,
    ny,
    src,
    frame_hbm,
    velocity_hbm,
    window_hbm,
    re_hbm,
    im_hbm,
    ere_hbm,
    eim_hbm,
    out,
    other,
    state,
    whole,
    partial,
    extra,
    extras,
    frames,
    velocities,
    width,
    products,
    mats,
    split_mats,
    picture,
    tiles,
    whole_tiles,
    rotors,
    re_ref,
    im_ref,
    ere_ref,
    eim_ref,
    operand_sem,
    send_sem,
    recv_sem,
    whole_send,
    whole_recv,
    extra_send,
    extra_recv,
    out_send,
    out_recv,
    whole_out_send,
    whole_out_recv,
):
    total_devices = nx * ny
    depth = ny // 2
    members = nx * depth
    my_x, my_y = lax.axis_index("sx"), lax.axis_index("sy")
    my_half = my_y // depth
    my_place = my_x * depth + lax.rem(my_y, depth)
    me = my_x * ny + my_y
    my_seat = my_x // 2 * ny + my_y
    seated = lax.rem(my_x, 2) == 0
    rows = src.shape[0]
    terms = rows // 2
    side = out.shape[0]

    def box_of(far, place):
        half = my_half + far - 2 * my_half * far
        return place // depth * ny + half * depth + lax.rem(place, depth)

    def coordinates(box):
        return box // ny, lax.rem(box, ny)

    def box_at(seat):
        return seat // ny * 2 * ny + lax.rem(seat, ny)

    def lanes_of(number):
        return pl.ds(pl.multiple_of(number * LANES, LANES), LANES)

    barrier = pltpu.get_barrier_semaphore()

    @pl.loop(1, total_devices)
    def _(step):
        peer = lax.rem(me + step, total_devices)
        pl.semaphore_signal(barrier, inc=1, device_id=coordinates(peer), device_id_type=MESH)

    loads = [
        pltpu.make_async_copy(hbm, ref, operand_sem.at[number])
        for number, (hbm, ref) in enumerate(
            [
                (frame_hbm, frames),
                (velocity_hbm, velocities),
                (window_hbm, width),
                (re_hbm, re_ref),
                (im_hbm, im_ref),
                (ere_hbm, ere_ref),
                (eim_hbm, eim_ref),
            ]
        )
    ]
    for load in loads:
        load.start()
    for load in loads[:3]:
        load.wait()
    points = velocities.shape[2]
    for number in range(total_devices):
        frame, offset = divmod(number * LANES, points)
        speeds = velocities[0, :, offset : offset + LANES]
        products[number : number + 1] = lax.rem(frames[0, 0, frame] * speeds, VGRID)
    angles = TWO_PI / VGRID * products[...].astype(jnp.float32)
    cosines, sines = jnp.cos(angles), jnp.sin(angles)
    widths = jnp.full((1, LANES), width[0, 0], jnp.int32).astype(jnp.float32)
    for number in range(total_devices):
        extra[number, :, 0:LANES] = cosines[number : number + 1]
        extra[number, :, LANES : 2 * LANES] = sines[number : number + 1]
        extra[number, :, 2 * LANES :] = widths
    pltpu.make_async_copy(
        src.at[:, lanes_of(my_place)], state.at[my_place], recv_sem.at[my_place]
    ).start()
    pltpu.make_async_copy(extra.at[my_place], extras.at[0, me], extra_recv.at[0, me]).start()

    @pl.when(seated)
    def _():
        number = members + my_seat
        pltpu.make_async_copy(
            src.at[:, lanes_of(number)], whole.at[me], whole_recv.at[me]
        ).start()
        pltpu.make_async_copy(extra.at[number], extras.at[1, me], extra_recv.at[1, me]).start()

    picture[...] = jnp.zeros_like(picture)

    pl.semaphore_wait(barrier, total_devices - 1)

    def send(source, target, sent, arrived, box):
        copy = pltpu.make_async_remote_copy(
            src_ref=source,
            dst_ref=target,
            send_sem=sent,
            recv_sem=arrived,
            device_id=coordinates(box),
            device_id_type=MESH,
        )
        copy.start()
        return copy

    sends = []
    for mask in range(1, members):
        place = flipped(my_place, mask, members)
        sends.append(
            send(
                src.at[:, lanes_of(place)],
                state.at[my_place],
                send_sem.at[mask],
                recv_sem.at[my_place],
                box_of(0, place),
            )
        )
    for far in range(2):
        for mask in range(1 - far, members):
            place = flipped(my_place, mask, members)
            sends.append(
                send(
                    extra.at[place],
                    extras.at[0, me],
                    extra_send.at[far, mask],
                    extra_recv.at[0, me],
                    box_of(far, place),
                )
            )

    def send_whole(mask):
        seat = flipped(my_seat, mask, members)
        number = members + seat
        return [
            send(
                src.at[:, lanes_of(number)],
                whole.at[me],
                whole_send.at[mask],
                whole_recv.at[me],
                box_at(seat),
            ),
            send(
                extra.at[number],
                extras.at[1, me],
                extra_send.at[2, mask],
                extra_recv.at[1, me],
                box_at(seat),
            ),
        ]

    half_mask = ny // 2
    for mask in sorted(range(1, members), key=lambda mask: (0 if mask & half_mask else 1, mask)):
        sends += send_whole(mask)

    @pl.when(jnp.logical_not(seated))
    def _():
        for copy in send_whole(0):
            copy.wait_send()

    for load in loads[3:]:
        load.wait()

    def put_matrix(target, top, left, level, bit, term):
        real = re_ref[level, bit, term]
        imag = im_ref[level, bit, term]
        target[top : top + terms, left : left + terms] = real
        target[top : top + terms, left + terms : left + rows] = -imag
        target[top + terms : top + rows, left : left + terms] = imag
        target[top + terms : top + rows, left + terms : left + rows] = real

    for level in range(LEVELS):
        if level == 1:
            put_matrix(split_mats, 0, 0, level, my_half, 0)
            put_matrix(split_mats, rows, 0, level, 1 - my_half, 1)
        for bit in range(2):
            put_matrix(mats.at[level], bit * rows, bit * rows, level, bit, 0)
            put_matrix(mats.at[level], bit * rows, (1 - bit) * rows, level, bit, 1)
    evaluate = jnp.concatenate([ere_ref[...], -eim_ref[...]], axis=1)

    def collect_rotors(kind):
        @pl.loop(0, total_devices)
        def _(box):
            block = extras.at[kind, box]
            pltpu.make_async_copy(block, block, extra_recv.at[kind, box]).wait()
            cosine = extras[kind, box, :, 0:LANES]
            sine = extras[kind, box, :, LANES : 2 * LANES]
            real, imag = cosine, sine
            for level in range(LEVELS):
                rotors[kind, level, 0, box] = real
                rotors[kind, level, 1, box] = imag
                if level + 1 < LEVELS:
                    real, imag = real * cosine - imag * sine, real * sine + imag * cosine

    def turned(piece, chunk, level, box):
        real, imag = piece[:terms], piece[terms:]
        cosine = rotors[chunk, level, 0, box]
        sine = rotors[chunk, level, 1, box]
        new_real = (cosine * real - sine * imag).astype(jnp.bfloat16)
        new_imag = (sine * real + cosine * imag).astype(jnp.bfloat16)
        return new_real, new_imag

    def exchange(boxes_ref, kind, level, box_at_index, width, group):
        axis_size = nx if level % 2 == 0 else ny
        stride = (width if level % 2 == 0 else 1) << (axis_size.bit_length() - 2 - level // 2)
        pairs = []
        for part in range(2):
            pair = 2 * group + part
            low = pair // stride * (2 * stride) + lax.rem(pair, stride)
            pairs.append((low, low + stride))
        stacked = jnp.concatenate(
            [jnp.concatenate([boxes_ref[low], boxes_ref[high]], axis=0) for low, high in pairs],
            axis=1,
        )
        sums = jnp.dot(mats[level], stacked, preferred_element_type=jnp.float32)
        for part, pair in enumerate(pairs):
            for bit, index in enumerate(pair):
                piece = sums[bit * rows : (bit + 1) * rows, part * LANES : (part + 1) * LANES]
                real, imag = turned(piece, kind, level, box_at_index(index))
                boxes_ref[index, 0:terms] = real
                boxes_ref[index, terms:rows] = imag

    def render(states, boxes):
        stacked = jnp.concatenate(states, axis=1)
        cells = jnp.dot(evaluate, stacked, preferred_element_type=jnp.float32)
        for part, box in enumerate(boxes):
            block = cells[:, part * LANES : (part + 1) * LANES].reshape(side, side, LANES)
            row, col = coordinates(box)
            picture[pl.ds(row * side + 2, side), col + 1] = block

    def smooth(box):
        row, col = coordinates(box)
        values = picture[pl.ds(row * side, side + 4), pl.ds(col, 3)]
        rows_near = values[1:-3] + values[2:-2] + values[3:-1]
        rows_far = rows_near + values[0:-4] + values[4:]
        rows_near = rows_near.reshape(side, 3 * side, LANES)
        rows_far = rows_far.reshape(side, 3 * side, LANES)

        def moved(block, shift):
            return block[:, side + shift : 2 * side + shift]

        box_near = moved(rows_near, -1) + moved(rows_near, 0) + moved(rows_near, 1)
        box_far = (
            moved(rows_far, -1)
            + moved(rows_far, 0)
            + moved(rows_far, 1)
            + moved(rows_far, -2)
            + moved(rows_far, 2)
        )
        wide = extras[0, box, :, 2 * LANES :].reshape(1, 1, LANES) == 2.0
        return jnp.where(wide, box_far / 25.0, box_near / 9.0).astype(jnp.bfloat16)

    def repeat(count, step):
        def body(index, _):
            step(index)
            return 0

        lax.fori_loop(0, count, body, 0, unroll=UNROLL)

    collect_rotors(0)

    @pl.loop(0, members)
    def _(place):
        block = state.at[place]
        pltpu.make_async_copy(block, block, recv_sem.at[place]).wait()

    repeat(
        members // 4, lambda group: exchange(state, 0, 0, lambda i: box_of(0, i), depth, group)
    )

    def split(group):
        places = [2 * group, 2 * group + 1]
        stacked = jnp.concatenate([state[place] for place in places], axis=1)
        sums = jnp.dot(split_mats[...], stacked, preferred_element_type=jnp.float32)
        for part, place in enumerate(places):
            for far in range(2):
                piece = sums[far * rows : (far + 1) * rows, part * LANES : (part + 1) * LANES]
                real, imag = turned(piece, 0, 1, box_of(far, place))
                partial[far, place, 0:terms] = real
                partial[far, place, terms:rows] = imag

    repeat(members // 2, split)
    for level in range(2, LEVELS):

        def later(group, level=level):
            for far in range(2):
                exchange(partial.at[far], 0, level, lambda i: box_of(far, i), depth, group)

        repeat(members // 4, later)
    repeat(
        members,
        lambda place: render(
            [partial[0, place], partial[1, place]], [box_of(0, place), box_of(1, place)]
        ),
    )
    for far in (1, 0):
        target = (other if far else out).at[:, :, lanes_of(my_place)]
        arrived = out_recv.at[far, my_place]
        for mask in range(members):
            place = flipped(my_place, mask, members)
            source = tiles.at[far, place]
            tiles[far, place] = smooth(box_of(far, place))
            if far == 0 and mask == 0:
                pltpu.make_async_copy(source, target, arrived).start()
            else:
                sent = out_send.at[far, mask]
                sends.append(send(source, target, sent, arrived, box_of(far, place)))

    @pl.when(seated)
    def _():
        collect_rotors(1)

        @pl.loop(0, total_devices)
        def _(box):
            block = whole.at[box]
            pltpu.make_async_copy(block, block, whole_recv.at[box]).wait()

        for level in range(LEVELS):
            repeat(
                total_devices // 4,
                lambda group, level=level: exchange(whole, 1, level, lambda i: i, ny, group),
            )
        repeat(
            total_devices // 2,
            lambda group: render(
                [whole[2 * group], whole[2 * group + 1]], [2 * group, 2 * group + 1]
            ),
        )
        target = out.at[:, :, lanes_of(members + my_seat)]
        arrived = whole_out_recv.at[my_seat]
        finals = []
        order = sorted(
            range(1, total_devices), key=lambda mask: (0 if mask & half_mask else 1, mask)
        )
        for mask in order:
            box = flipped(me, mask, total_devices)
            whole_tiles[box] = smooth(box).astype(jnp.bfloat16)
            sent = whole_out_send.at[mask]
            finals.append(send(whole_tiles.at[box], target, sent, arrived, box))
        whole_tiles[me] = smooth(me)
        pltpu.make_async_copy(whole_tiles.at[me], target, arrived).start()
        for copy in finals:
            copy.wait_send()

    for copy in sends:
        copy.wait_send()

    @pl.loop(0, members)
    def _(place):
        for far in range(2):
            block = tiles.at[far, place]
            pltpu.make_async_copy(block, block, out_recv.at[far, place]).wait()
        block = whole_tiles.at[place]
        pltpu.make_async_copy(block, block, whole_out_recv.at[place]).wait()


def spread_on_device(
    nx,
    ny,
    sources,
    translate_re,
    translate_im,
    frame_index,
    velocity_index,
    eval_re,
    eval_im,
    window,
):
    total_devices = nx * ny
    members = total_devices // 2
    terms, columns = sources.shape[3:]
    rows = 2 * terms
    side = math.isqrt(eval_re.shape[0])
    anywhere = pl.BlockSpec(memory_space=pl.ANY)
    dma = pltpu.SemaphoreType.DMA
    vmem = pltpu.VMEM
    out, other = pl.pallas_call(
        functools.partial(spread_kernel, nx, ny),
        out_shape=(
            jax.ShapeDtypeStruct((side, side, columns), jnp.bfloat16),
            jax.ShapeDtypeStruct((side, side, members * LANES), jnp.bfloat16),
        ),
        in_specs=[anywhere] * 8,
        out_specs=(anywhere, anywhere),
        scratch_shapes=[
            vmem((members, rows, LANES), jnp.bfloat16),
            vmem((total_devices, rows, LANES), jnp.bfloat16),
            vmem((2, members, rows, LANES), jnp.bfloat16),
            vmem((total_devices, 1, 3 * LANES), jnp.float32),
            vmem((2, total_devices, 1, 3 * LANES), jnp.float32),
            pltpu.SMEM(frame_index.shape, jnp.int32),
            vmem(velocity_index.shape, jnp.int32),
            pltpu.SMEM(window.shape, jnp.int32),
            vmem((total_devices, LANES), jnp.int32),
            vmem((LEVELS, 2 * rows, 2 * rows), jnp.bfloat16),
            vmem((2 * rows, rows), jnp.bfloat16),
            vmem((nx * side + 4, ny + 2, side, LANES), jnp.float32),
            vmem((2, members, side, side, LANES), jnp.bfloat16),
            vmem((total_devices, side, side, LANES), jnp.bfloat16),
            vmem((2, LEVELS, 2, total_devices, 1, LANES), jnp.float32),
            vmem(translate_re.shape, jnp.bfloat16),
            vmem(translate_im.shape, jnp.bfloat16),
            vmem(eval_re.shape, jnp.bfloat16),
            vmem(eval_im.shape, jnp.bfloat16),
            dma((7,)),
            dma((members,)),
            dma((members,)),
            dma((members,)),
            dma((total_devices,)),
            dma((3, members)),
            dma((2, total_devices)),
            dma((2, members)),
            dma((2, members)),
            dma((total_devices,)),
            dma((members,)),
        ],
        compiler_params=pltpu.CompilerParams(collective_id=0, has_side_effects=True),
    )(
        sources[0, 0].reshape(rows, columns),
        frame_index,
        velocity_index,
        window,
        translate_re,
        translate_im,
        eval_re,
        eval_im,
    )
    other = jnp.pad(other, ((0, 0), (0, 0), (0, columns - other.shape[2])))
    return (out.astype(jnp.float32) + other.astype(jnp.float32)).astype(jnp.bfloat16)


def solution(mesh):
    nx, ny = mesh.shape["sx"], mesh.shape["sy"]

    def body(sources, *others):
        fits = others[3].shape[2] % LANES == 0
        if fits and sources.shape[4] == nx * ny * LANES:
            return spread_on_device(nx, ny, sources, *others)
        return on_device(sources, *others)

    return jax.shard_map(
        body,
        mesh=mesh,
        in_specs=(
            P("sx", "sy", None, None, None),
            P(),
            P(),
            P("sx", "sy", None),
            P("sx", "sy", None),
            P(),
            P(),
            P("sx", "sy"),
        ),
        out_specs=P("sx", "sy", None),
        check_vma=False,
    )
```
